32 devices in a mesh: grp: 2 (over x), ctx: 4 (over y, core), head: 4 (over z).
Axes of the slice: x: 2, y: 2, z: 4, core: 2. Of those that a mesh axis runs over, the one named last changes fastest.
Arguments:
- queries: bfloat16 [8192, 4096], P(('grp', 'ctx'), 'head'), parts along dimension 0, may hold values from -6 to 6
- keys: bfloat16 [8192, 4096], P(('grp', 'ctx'), 'head'), parts along dimension 0, may hold values from -6 to 6
- values: bfloat16 [8192, 4096], P(('grp', 'ctx'), 'head'), parts along dimension 0, may hold values from -6 to 6
- init_state: float32 [64, 128, 128], P(('grp', 'head')), parts along dimension 0, may hold values from -192 to 192
- out_grad: bfloat16 [8192, 4096], P(('grp', 'ctx'), 'head'), parts along dimension 0, may hold values from -6 to 6
Outputs:
- output: bfloat16 [8192, 4096], P(('grp', 'ctx'), 'head'), parts along dimension 0
- query_grad: bfloat16 [8192, 4096], P(('grp', 'ctx'), 'head'), parts along dimension 0
- key_grad: bfloat16 [8192, 4096], P(('grp', 'ctx'), 'head'), parts along dimension 0
- value_grad: bfloat16 [8192, 4096], P(('grp', 'ctx'), 'head'), parts along dimension 0
- state_grad: float32 [64, 128, 128], P(('grp', 'head')), parts along dimension 0
The draws below stay inside these ranges and needn't reach their ends.
There are 2 independent parts, one for each index of `grp`. The reference program is written for one: setup_inputs(seed, part) draws one part's arguments, and reference() takes and returns one part's arrays. A program takes and returns all parts, laid end to end along the dimension named above; each array names one. Nothing has to cross between parts.
All inputs are finite; a program needn't handle non-finite values.
Results may differ from the reference program's by a relative error of at most 0.0058.
Values sent between devices are 32-bit elements; how exact they have to be, the bound alone decides.
A program may use at most 128 MiB of HBM per device.

```python
import jax
import jax.numpy as jnp
from jax import lax

HEADS = 32
HEAD_DIM = 128
TOK_DEV = 1024
WIDTH = 4096
TOKENS = 4096


def steps_of(own_key, extent, shards, low, largest):
    def one(axis_at, blocks):
        heights = jax.random.uniform(jax.random.fold_in(jax.random.fold_in(own_key, 6), axis_at), (blocks,), jnp.float32, low / len(shards), largest / len(shards))
        return jnp.repeat(jnp.exp(heights), extent[axis_at] // blocks).reshape((-1,) + (1,) * (len(extent) - axis_at - 1))

    level = one(*shards[0])
    for cut in shards[1:]:
        level = level * one(*cut)
    return level


def centred(key, shape, scale, reach, shards=(), kind=jnp.bfloat16):
    level = steps_of(key, shape, shards, -0.22, 0.18) if shards else 1.0
    drawn = jax.random.normal(key, shape, jnp.float32) * scale * level
    return jnp.minimum(jnp.maximum(drawn, -reach), reach).astype(kind)


def setup_inputs(seed: int = 0, part: int = 0) -> dict:
    key_of = jax.random.split(jax.random.key(seed), 6)
    own_keys = jax.random.split(jax.random.fold_in(key_of[5], part), 6)
    return {
        "queries": centred(own_keys[0], (TOKENS, WIDTH), 1.0, 6.0, ((0, 4), (1, 4))),
        "keys": centred(own_keys[1], (TOKENS, WIDTH), 1.0, 6.0, ((0, 4), (1, 4))),
        "values": centred(own_keys[2], (TOKENS, WIDTH), 1.0, 6.0, ((0, 4), (1, 4))),
        "init_state": centred(own_keys[3], (HEADS, HEAD_DIM, HEAD_DIM), (max(1, TOK_DEV // 32)), 192.0, ((0, 4),), jnp.float32),
        "out_grad": centred(own_keys[4], (TOKENS, WIDTH), 1.0, 6.0, ((0, 4), (1, 4))),
    }


def round_half(x):
    return lax.optimization_barrier(x.astype(jnp.bfloat16)).astype(jnp.float32)

def reference(queries, keys, values, init_state, out_grad):
    blocks = queries.shape[0] // TOK_DEV
    shape = (blocks, TOK_DEV, HEADS, HEAD_DIM)
    q_all = queries.astype(jnp.float32).reshape(shape)
    k_all = keys.astype(jnp.float32).reshape(shape)
    v_all = values.astype(jnp.float32).reshape(shape)
    g_all = out_grad.astype(jnp.float32).reshape(shape)
    causal = jnp.arange(TOK_DEV)[:, None] >= jnp.arange(TOK_DEV)[None, :]
    block_state = jnp.einsum('cthd,cthe->chde', k_all, v_all)
    zero_state = jnp.zeros((1, HEADS, HEAD_DIM, HEAD_DIM), jnp.float32)
    earlier = jnp.concatenate([zero_state, jnp.cumsum(block_state, axis=0)[:-1]], axis=0)
    prefix_b = round_half(init_state[None] + earlier)

    def forward_block(items):
        q_blk, k_blk, v_blk, p_blk, g_blk = items
        raw = jnp.einsum('thd,shd->hts', q_blk, k_blk)
        scores = round_half(jnp.where(causal[None], raw, 0.0))
        attended = jnp.einsum('thd,hde->the', q_blk, p_blk) + jnp.einsum('hts,she->the', scores, v_blk)
        inv_rms = lax.rsqrt(lax.optimization_barrier(jnp.mean(attended * attended, axis=-1, keepdims=True)) + 1e-06)
        normed = attended * inv_rms
        grad_att = round_half(inv_rms * (g_blk - normed * lax.optimization_barrier(jnp.mean(g_blk * normed, axis=-1, keepdims=True))))
        block_grad = jnp.einsum('thd,the->hde', q_blk, grad_att)
        return (normed.astype(jnp.bfloat16), grad_att, block_grad)
    output, grad_att, block_grad = lax.map(forward_block, (q_all, k_all, v_all, prefix_b, g_all))
    later = jnp.concatenate([jnp.cumsum(block_grad[::-1], axis=0)[::-1][1:], zero_state], axis=0)
    suffix_b = round_half(later)
    state_grad = lax.optimization_barrier(jnp.sum(block_grad, axis=0))

    def backward_block(items):
        q_blk, k_blk, v_blk, p_blk, s_blk, d_blk = items
        raw = jnp.einsum('thd,shd->hts', q_blk, k_blk)
        scores = round_half(jnp.where(causal[None], raw, 0.0))
        grad_scores = round_half(jnp.where(causal[None], jnp.einsum('the,she->hts', d_blk, v_blk), 0.0))
        q_grad = jnp.einsum('the,hde->thd', d_blk, p_blk) + jnp.einsum('hts,shd->thd', grad_scores, k_blk)
        k_grad = jnp.einsum('hts,thd->shd', grad_scores, q_blk) + jnp.einsum('she,hde->shd', v_blk, s_blk)
        v_grad = jnp.einsum('hts,the->she', scores, d_blk) + jnp.einsum('shd,hde->she', k_blk, s_blk)
        return (q_grad.astype(jnp.bfloat16), k_grad.astype(jnp.bfloat16), v_grad.astype(jnp.bfloat16))
    query_grad, key_grad, value_grad = lax.map(backward_block, (q_all, k_all, v_all, prefix_b, suffix_b, grad_att))
    flat = (blocks * TOK_DEV, HEADS * HEAD_DIM)
    return (output.reshape(flat), query_grad.reshape(flat), key_grad.reshape(flat), value_grad.reshape(flat), state_grad)
```

```python
import functools

import jax
import jax.numpy as jnp
from jax import lax
from jax.experimental import pallas as pl
from jax.experimental.pallas import tpu as pltpu
from jax.sharding import PartitionSpec as P

F32 = jnp.float32
BF16 = jnp.bfloat16
MESH = pl.DeviceIdType.MESH
CHUNK = 256


def nn(a, b):
    return lax.dot_general(a, b, (((1,), (0,)), ((), ())), preferred_element_type=F32)


def nt(a, b):
    return lax.dot_general(a, b, (((1,), (1,)), ((), ())), preferred_element_type=F32)


def tn(a, b):
    return lax.dot_general(a, b, (((0,), (0,)), ((), ())), preferred_element_type=F32)


def kernel(
    n, heads, dim, rows,
    q_hbm, k_hbm, v_hbm, i_hbm, g_hbm,
    out, dq, dk, dv, sg,
    q, k, v, g, init, acc_a, acc_b, score, da, cum, gcum, pre, state, grad,
    p1_in, p2_out, p2_in, p3_out, p3_in,
    b1_in, b2_out, b2_in, b3_out, b3_in, t_out, t_in,
    sem_in, sem_init, one_send, one_recv, two_send, two_recv,
):
    gh = heads // 2
    chips = n // 2
    chunks = rows // CHUNK
    me = lax.axis_index("ctx")
    core = lax.rem(me, 2)
    chip = me // 2
    partner = me + 1 - 2 * core
    peers = [2 * lax.rem(chip + j, chips) + core for j in range(1, chips)]
    mine = core * gh
    other = (1 - core) * gh

    barrier = pltpu.get_barrier_semaphore()
    for device in [partner] + peers:
        pl.semaphore_signal(barrier, inc=1, device_id={"ctx": device}, device_id_type=MESH)

    def strip(h):
        return pl.ds(pl.multiple_of(h * dim, dim), dim)

    def load(which, h):
        src, dst = ((k_hbm, k), (v_hbm, v), (q_hbm, q), (g_hbm, g))[which]
        return pltpu.make_async_copy(
            src.at[:, strip(h)], dst.at[:, strip(h)], sem_in.at[which, h]
        )

    load_init = pltpu.make_async_copy(i_hbm, init, sem_init)

    def issue(first, kinds):
        def step(i, _):
            h = lax.rem(first + i, heads)
            for kind in kinds:
                load(kind, h).start()
            return 0

        lax.fori_loop(0, heads, step, 0)

    issue(other, (0, 1))
    issue(other, (2,))
    load_init.start()
    issue(mine, (3,))
    pl.semaphore_wait(barrier, chips)

    def to_partner(which, src, dst, i):
        return pltpu.make_async_remote_copy(
            src_ref=src, dst_ref=dst,
            send_sem=one_send.at[which, i], recv_sem=one_recv.at[which, i],
            device_id={"ctx": partner}, device_id_type=MESH,
        )

    def to_peer(which, j, src, dst, i):
        return pltpu.make_async_remote_copy(
            src_ref=src, dst_ref=dst,
            send_sem=two_send.at[which, j, i], recv_sem=two_recv.at[which, j, i],
            device_id={"ctx": peers[j]}, device_id_type=MESH,
        )

    def p1(i):
        return to_partner(0, state.at[other + i], p1_in.at[i], i)

    def p2(j, i):
        return to_peer(0, j, p2_out.at[i], p2_in.at[j, i], i)

    def p3(i):
        return to_partner(1, p3_out.at[i], p3_in.at[i], i)

    def b1(i):
        return to_partner(2, grad.at[mine + i], b1_in.at[i], i)

    def b2(j, i):
        return to_peer(1, j, b2_out.at[i], b2_in.at[j, i], i)

    def b3(i):
        return to_partner(3, b3_out.at[i], b3_in.at[i], i)

    def bt(i):
        return to_partner(4, t_out.at[i], t_in.at[i], i)

    def rc(c):
        return pl.ds(c * CHUNK, CHUNK)

    def states(h):
        load(0, h).wait()
        load(1, h).wait()
        total = jnp.zeros((dim, dim), F32)
        for c in range(chunks):
            cum[h, c] = total
            total = total + tn(k[rc(c), strip(h)], v[rc(c), strip(h)])
        state[h] = total

    def states_other(i, _):
        states(other + i)
        p1(i).start()
        return 0

    lax.fori_loop(0, gh, states_other, 0)

    def states_mine(i, _):
        states(mine + i)
        p1(i).wait_recv()
        p2_out[i] = state[mine + i] + p1_in[i]
        for j in range(chips - 1):
            p2(j, i).start()
        return 0

    lax.fori_loop(0, gh, states_mine, 0)

    causal = lax.broadcasted_iota(jnp.int32, (CHUNK, CHUNK), 0) >= lax.broadcasted_iota(
        jnp.int32, (CHUNK, CHUNK), 1
    )

    def within(i, _):
        h = lax.rem(other + i, heads)
        load(2, h).wait()
        for c in range(chunks):
            raw = nt(q[rc(c), strip(h)], k[rc(c), strip(h)])
            s = jnp.where(causal, raw, 0.0).astype(BF16)
            score[h, c] = s
            acc_a[rc(c), strip(h)] = nn(s, v[rc(c), strip(h)])
        return 0

    lax.fori_loop(0, heads, within, 0)
    load_init.wait()

    def forward(h, prefix):
        load(3, h).wait()
        total = jnp.zeros((dim, dim), F32)
        for c in range(chunks):
            at = (rc(c), strip(h))
            p_b = (prefix + cum[h, c]).astype(BF16)
            pre[h, c] = p_b
            q_c = q[at]
            a = acc_a[at] + nn(q_c, p_b)
            inv = lax.rsqrt(jnp.mean(a * a, axis=-1, keepdims=True) + 1e-06)
            normed = a * inv
            out[at] = normed.astype(BF16)
            up = g[at].astype(F32)
            d = (inv * (up - normed * jnp.mean(up * normed, axis=-1, keepdims=True))).astype(BF16)
            da[at] = d
            part = tn(q_c, d)
            gcum[h, c] = part
            total = total + part
        grad[h] = total

    zero = jnp.zeros((dim, dim), F32)

    def forward_mine(i, _):
        h = mine + i
        before = zero
        for j in range(chips - 1):
            p2(j, i).wait_recv()
            before = before + jnp.where(chip >= j + 1, p2_in[j, i], 0.0)
        p3_out[i] = before + jnp.where(core == 0, state[h], 0.0)
        p3(i).start()
        forward(h, init[h] + before + jnp.where(core == 1, p1_in[i], 0.0))
        b1(i).start()
        return 0

    lax.fori_loop(0, gh, forward_mine, 0)

    def forward_other(i, _):
        h = other + i
        p3(i).wait_recv()
        forward(h, init[h] + p3_in[i])
        b1(i).wait_recv()
        b2_out[i] = grad[h] + b1_in[i]
        for j in range(chips - 1):
            b2(j, i).start()
        return 0

    lax.fori_loop(0, gh, forward_other, 0)

    def backward(i, _):
        h = lax.rem(mine + i, heads)
        for c in range(chunks):
            at = (rc(c), strip(h))
            d = da[at]
            raw = nt(d, v[at])
            ds = jnp.where(causal, raw, 0.0).astype(BF16)
            dq[at] = (nt(d, pre[h, c]) + nn(ds, k[at])).astype(BF16)
            acc_a[at] = tn(ds, q[at])
            acc_b[at] = tn(score[h, c], d)
        return 0

    split = heads - heads // 4
    lax.fori_loop(0, split, backward, 0)

    def relay(i, _):
        h = other + i
        total = b2_out[i]
        after = zero
        for j in range(chips - 1):
            b2(j, i).wait_recv()
            total = total + b2_in[j, i]
            after = after + jnp.where(chip >= j + 1, 0.0, b2_in[j, i])
        b3_out[i] = after + jnp.where(core == 1, grad[h], 0.0)
        b3(i).start()
        t_out[i] = total
        bt(i).start()
        sg[h] = total
        b2_out_later = after + jnp.where(core == 0, b1_in[i], 0.0)
        grad[h] = b2_out_later
        return 0

    lax.fori_loop(0, gh, relay, 0)
    lax.fori_loop(split, heads, backward, 0)

    def finish(h, suffix):
        for c in reversed(range(chunks)):
            at = (rc(c), strip(h))
            s_b = suffix.astype(BF16)
            dk[at] = (acc_a[at] + nt(v[at], s_b)).astype(BF16)
            dv[at] = (acc_b[at] + nn(k[at], s_b)).astype(BF16)
            if c:
                suffix = suffix + gcum[h, c]

    def finish_other(i, _):
        finish(other + i, grad[other + i])
        return 0

    lax.fori_loop(0, gh, finish_other, 0)

    def finish_mine(i, _):
        b3(i).wait_recv()
        finish(mine + i, b3_in[i])
        bt(i).wait_recv()
        sg[mine + i] = t_in[i]
        return 0

    lax.fori_loop(0, gh, finish_mine, 0)

    def drain(i, _):
        p1(i).wait_send()
        p3(i).wait_send()
        b1(i).wait_send()
        b3(i).wait_send()
        bt(i).wait_send()
        for j in range(chips - 1):
            p2(j, i).wait_send()
            b2(j, i).wait_send()
        return 0

    lax.fori_loop(0, gh, drain, 0)


def shards(n, queries, keys, values, init_state, out_grad):
    rows, width = queries.shape
    heads, dim, _ = init_state.shape
    gh = heads // 2
    chips = n // 2
    chunks = rows // CHUNK
    far = max(chips - 1, 1)
    flat = pltpu.VMEM((rows, width), BF16)
    group = pltpu.VMEM((gh, dim, dim), F32)
    every = pltpu.VMEM((heads, dim, dim), F32)
    peers = pltpu.VMEM((far, gh, dim, dim), F32)
    dma = pltpu.SemaphoreType.DMA
    return pl.pallas_call(
        functools.partial(kernel, n, heads, dim, rows),
        out_shape=[pltpu.VMEM((rows, width), BF16)] * 4 + [pltpu.VMEM((heads, dim, dim), F32)],
        in_specs=[pl.BlockSpec(memory_space=pl.ANY)] * 5,
        out_specs=[pl.BlockSpec(memory_space=pltpu.VMEM)] * 5,
        scratch_shapes=[
            flat, flat, flat, flat, every,
            pltpu.VMEM((rows, width), F32),
            pltpu.VMEM((rows, width), F32),
            pltpu.VMEM((heads, chunks, CHUNK, CHUNK), BF16),
            flat,
            pltpu.VMEM((heads, chunks, dim, dim), F32),
            pltpu.VMEM((heads, chunks, dim, dim), F32),
            pltpu.VMEM((heads, chunks, dim, dim), BF16),
            every, every,
            group, group, peers, group, group,
            group, group, peers, group, group, group, group,
            dma((4, heads)), dma,
            dma((5, gh)), dma((5, gh)),
            dma((2, far, gh)), dma((2, far, gh)),
        ],
        compiler_params=pltpu.CompilerParams(
            collective_id=0, has_side_effects=True, vmem_limit_bytes=50 * 1024 * 1024
        ),
    )(queries, keys, values, init_state, out_grad)


def solution(mesh):
    tokens = P(("grp", "ctx"), "head")
    states = P(("grp", "head"), None, None)
    return jax.shard_map(
        functools.partial(shards, mesh.shape["ctx"]),
        mesh=mesh,
        in_specs=(tokens, tokens, tokens, states, tokens),
        out_specs=(tokens, tokens, tokens, tokens, states),
        check_vma=False,
    )
```

```python
import functools

import jax
import jax.numpy as jnp
from jax import lax
from jax.experimental import pallas as pl
from jax.experimental.pallas import tpu as pltpu
from jax.sharding import PartitionSpec as P

F32 = jnp.float32
BF16 = jnp.bfloat16
MESH = pl.DeviceIdType.MESH
CHUNK = 256


def nn(a, b):
    return lax.dot_general(a, b, (((1,), (0,)), ((), ())), preferred_element_type=F32)


def nt(a, b):
    return lax.dot_general(a, b, (((1,), (1,)), ((), ())), preferred_element_type=F32)


def tn(a, b):
    return lax.dot_general(a, b, (((0,), (0,)), ((), ())), preferred_element_type=F32)


def kernel(
    n, heads, dim, rows,
    q_hbm, k_hbm, v_hbm, i_hbm, g_hbm,
    out, dq, sg, k, v, acc_a, acc_b, suf,
    q, g, init, score, da, cum, gcum, pre, state, grad,
    p1_in, p2_out, p2_in, p3_out, p3_in,
    b1_in, b2_out, b2_in, b3_out, b3_in, t_out, t_in,
    sem_in, sem_init, one_send, one_recv, two_send, two_recv,
):
    gh = heads // 2
    chips = n // 2
    chunks = rows // CHUNK
    me = lax.axis_index("ctx")
    core = lax.rem(me, 2)
    chip = me // 2
    partner = me + 1 - 2 * core
    peers = [2 * lax.rem(chip + j, chips) + core for j in range(1, chips)]
    mine = core * gh
    other = (1 - core) * gh

    barrier = pltpu.get_barrier_semaphore()
    for device in [partner] + peers:
        pl.semaphore_signal(barrier, inc=1, device_id={"ctx": device}, device_id_type=MESH)

    def strip(h):
        return pl.ds(pl.multiple_of(h * dim, dim), dim)

    def load(which, h):
        src, dst = ((k_hbm, k), (v_hbm, v), (q_hbm, q), (g_hbm, g))[which]
        return pltpu.make_async_copy(
            src.at[:, strip(h)], dst.at[:, strip(h)], sem_in.at[which, h]
        )

    load_init = pltpu.make_async_copy(i_hbm, init, sem_init)

    def issue(first, kinds):
        def step(i, _):
            h = lax.rem(first + i, heads)
            for kind in kinds:
                load(kind, h).start()
            return 0

        lax.fori_loop(0, heads, step, 0)

    issue(other, (0, 1))
    issue(other, (2,))
    load_init.start()
    issue(mine, (3,))
    pl.semaphore_wait(barrier, chips)

    def to_partner(which, src, dst, i):
        return pltpu.make_async_remote_copy(
            src_ref=src, dst_ref=dst,
            send_sem=one_send.at[which, i], recv_sem=one_recv.at[which, i],
            device_id={"ctx": partner}, device_id_type=MESH,
        )

    def to_peer(which, j, src, dst, i):
        return pltpu.make_async_remote_copy(
            src_ref=src, dst_ref=dst,
            send_sem=two_send.at[which, j, i], recv_sem=two_recv.at[which, j, i],
            device_id={"ctx": peers[j]}, device_id_type=MESH,
        )

    def p1(i):
        return to_partner(0, state.at[other + i], p1_in.at[i], i)

    def p2(j, i):
        return to_peer(0, j, p2_out.at[i], p2_in.at[j, i], i)

    def p3(i):
        return to_partner(1, p3_out.at[i], p3_in.at[i], i)

    def b1(i):
        return to_partner(2, grad.at[mine + i], b1_in.at[i], i)

    def b2(j, i):
        return to_peer(1, j, b2_out.at[i], b2_in.at[j, i], i)

    def b3(i):
        return to_partner(3, b3_out.at[i], b3_in.at[i], i)

    def bt(i):
        return to_partner(4, t_out.at[i], t_in.at[i], i)

    def rc(c):
        return pl.ds(c * CHUNK, CHUNK)

    def states(h):
        load(0, h).wait()
        load(1, h).wait()
        parts = [tn(k[rc(c), strip(h)], v[rc(c), strip(h)]) for c in range(chunks)]
        total = jnp.zeros((dim, dim), F32)
        for c in range(chunks):
            cum[h, c] = total
            total = total + parts[c]
        state[h] = total

    def states_other(i, _):
        states(other + i)
        p1(i).start()
        return 0

    lax.fori_loop(0, gh, states_other, 0)

    def states_mine(i, _):
        states(mine + i)
        p1(i).wait_recv()
        p2_out[i] = state[mine + i] + p1_in[i]
        for j in range(chips - 1):
            p2(j, i).start()
        return 0

    lax.fori_loop(0, gh, states_mine, 0)

    causal = lax.broadcasted_iota(jnp.int32, (CHUNK, CHUNK), 0) >= lax.broadcasted_iota(
        jnp.int32, (CHUNK, CHUNK), 1
    )

    def within(i, _):
        h = lax.rem(other + i, heads)
        load(2, h).wait()
        held = []
        for c in range(chunks):
            raw = nt(q[rc(c), strip(h)], k[rc(c), strip(h)])
            held.append(jnp.where(causal, raw, 0.0).astype(BF16))
            score[h, c] = held[c]
        for c in range(chunks):
            acc_a[rc(c), strip(h)] = nn(held[c], v[rc(c), strip(h)])
        return 0

    lax.fori_loop(0, heads, within, 0)
    load_init.wait()

    def forward(h, prefix):
        load(3, h).wait()
        held = []
        for c in range(chunks):
            at = (rc(c), strip(h))
            pre[h, c] = (prefix + cum[h, c]).astype(BF16)
            held.append(acc_a[at] + nn(q[at], pre[h, c]))
        scale = [
            lax.rsqrt(jnp.mean(a * a, axis=-1, keepdims=True) + 1e-06) for a in held
        ]
        held = [a * inv for a, inv in zip(held, scale)]
        rise = []
        for c in range(chunks):
            at = (rc(c), strip(h))
            out[at] = held[c].astype(BF16)
            rise.append(g[at].astype(F32))
        along = [jnp.mean(u * x, axis=-1, keepdims=True) for u, x in zip(rise, held)]
        for c in range(chunks):
            da[rc(c), strip(h)] = (scale[c] * (rise[c] - held[c] * along[c])).astype(BF16)
        parts = [tn(q[rc(c), strip(h)], da[rc(c), strip(h)]) for c in range(chunks)]
        total = parts[0]
        for part in parts[1:]:
            total = total + part
        grad[h] = total
        for c in range(chunks):
            gcum[h, c] = parts[c]

    zero = jnp.zeros((dim, dim), F32)

    def forward_mine(i, _):
        h = mine + i
        before = zero
        for j in range(chips - 1):
            p2(j, i).wait_recv()
            before = before + jnp.where(chip >= j + 1, p2_in[j, i], 0.0)
        p3_out[i] = before + jnp.where(core == 0, state[h], 0.0)
        p3(i).start()
        forward(h, init[h] + before + jnp.where(core == 1, p1_in[i], 0.0))
        b1(i).start()
        return 0

    lax.fori_loop(0, gh, forward_mine, 0)

    def forward_other(i, _):
        h = other + i
        p3(i).wait_recv()
        forward(h, init[h] + p3_in[i])
        b1(i).wait_recv()
        b2_out[i] = grad[h] + b1_in[i]
        for j in range(chips - 1):
            b2(j, i).start()
        return 0

    lax.fori_loop(0, gh, forward_other, 0)

    def backward(i, _):
        h = lax.rem(mine + i, heads)
        held = []
        for c in range(chunks):
            at = (rc(c), strip(h))
            raw = nt(da[at], v[at])
            held.append(jnp.where(causal, raw, 0.0).astype(BF16))
        for c in range(chunks):
            at = (rc(c), strip(h))
            acc_b[at] = tn(score[h, c], da[at])
        for c in range(chunks):
            at = (rc(c), strip(h))
            dq[at] = (nt(da[at], pre[h, c]) + nn(held[c], k[at])).astype(BF16)
        for c in range(chunks):
            at = (rc(c), strip(h))
            acc_a[at] = tn(held[c], q[at])
        return 0

    split = heads - heads // 4
    lax.fori_loop(0, split, backward, 0)

    def relay(i, _):
        h = other + i
        total = b2_out[i]
        after = zero
        for j in range(chips - 1):
            b2(j, i).wait_recv()
            total = total + b2_in[j, i]
            after = after + jnp.where(chip >= j + 1, 0.0, b2_in[j, i])
        b3_out[i] = after + jnp.where(core == 1, grad[h], 0.0)
        b3(i).start()
        t_out[i] = total
        bt(i).start()
        sg[h] = total
        b2_out_later = after + jnp.where(core == 0, b1_in[i], 0.0)
        grad[h] = b2_out_later
        return 0

    lax.fori_loop(0, gh, relay, 0)
    lax.fori_loop(split, heads, backward, 0)

    def finish(h, suffix):
        for c in reversed(range(chunks)):
            suf[h, c] = suffix.astype(BF16)
            if c:
                suffix = suffix + gcum[h, c]

    def finish_other(i, _):
        finish(other + i, grad[other + i])
        return 0

    lax.fori_loop(0, gh, finish_other, 0)

    def finish_mine(i, _):
        b3(i).wait_recv()
        finish(mine + i, b3_in[i])
        bt(i).wait_recv()
        sg[mine + i] = t_in[i]
        return 0

    lax.fori_loop(0, gh, finish_mine, 0)

    def drain(i, _):
        p1(i).wait_send()
        p3(i).wait_send()
        b1(i).wait_send()
        b3(i).wait_send()
        bt(i).wait_send()
        for j in range(chips - 1):
            p2(j, i).wait_send()
            b2(j, i).wait_send()
        return 0

    lax.fori_loop(0, gh, drain, 0)


def tail(
    heads, dim, rows,
    out, dq, sg, k, v, acc_a, acc_b, suf,
    out_hbm, dq_hbm, dk_hbm, dv_hbm, sg_hbm,
    dk, dv, sem_whole, sem_head,
):
    chunks = rows // CHUNK
    whole = [
        pltpu.make_async_copy(src, dst, sem_whole.at[i])
        for i, (src, dst) in enumerate(((out, out_hbm), (dq, dq_hbm), (sg, sg_hbm)))
    ]
    for copy in whole:
        copy.start()

    def strip(h):
        return pl.ds(pl.multiple_of(h * dim, dim), dim)

    def store(which, h):
        src, dst = ((dk, dk_hbm), (dv, dv_hbm))[which]
        return pltpu.make_async_copy(
            src.at[:, strip(h)], dst.at[:, strip(h)], sem_head.at[which, h]
        )

    def finish(h, _):
        for c in range(chunks):
            at = (pl.ds(c * CHUNK, CHUNK), strip(h))
            s_b = suf[h, c]
            dk[at] = (acc_a[at] + nt(v[at], s_b)).astype(BF16)
            dv[at] = (acc_b[at] + nn(k[at], s_b)).astype(BF16)
        store(0, h).start()
        store(1, h).start()
        return 0

    lax.fori_loop(0, heads, finish, 0)

    def drain(h, _):
        store(0, h).wait()
        store(1, h).wait()
        return 0

    lax.fori_loop(0, heads, drain, 0)
    for copy in whole:
        copy.wait()


def shards(n, queries, keys, values, init_state, out_grad):
    rows, width = queries.shape
    heads, dim, _ = init_state.shape
    gh = heads // 2
    chips = n // 2
    chunks = rows // CHUNK
    far = max(chips - 1, 1)
    flat = pltpu.VMEM((rows, width), BF16)
    wide = pltpu.VMEM((rows, width), F32)
    group = pltpu.VMEM((gh, dim, dim), F32)
    every = pltpu.VMEM((heads, dim, dim), F32)
    peers = pltpu.VMEM((far, gh, dim, dim), F32)
    dma = pltpu.SemaphoreType.DMA
    held = pl.pallas_call(
        functools.partial(kernel, n, heads, dim, rows),
        out_shape=[
            flat, flat, every, flat, flat, wide, wide,
            pltpu.VMEM((heads, chunks, dim, dim), BF16),
        ],
        in_specs=[pl.BlockSpec(memory_space=pltpu.HBM)] * 5,
        out_specs=[pl.BlockSpec(memory_space=pltpu.VMEM)] * 8,
        scratch_shapes=[
            flat, flat, every,
            pltpu.VMEM((heads, chunks, CHUNK, CHUNK), BF16),
            flat,
            pltpu.VMEM((heads, chunks, dim, dim), F32),
            pltpu.VMEM((heads, chunks, dim, dim), F32),
            pltpu.VMEM((heads, chunks, dim, dim), BF16),
            every, every,
            group, group, peers, group, group,
            group, group, peers, group, group, group, group,
            dma((4, heads)), dma,
            dma((5, gh)), dma((5, gh)),
            dma((2, far, gh)), dma((2, far, gh)),
        ],
        compiler_params=pltpu.CompilerParams(
            collective_id=0, has_side_effects=True, vmem_limit_bytes=46 * 1024 * 1024
        ),
    )(queries, keys, values, init_state, out_grad)
    flat_out = jax.ShapeDtypeStruct((rows, width), BF16)
    return pl.pallas_call(
        functools.partial(tail, heads, dim, rows),
        out_shape=[flat_out] * 4 + [jax.ShapeDtypeStruct((heads, dim, dim), F32)],
        in_specs=[pl.BlockSpec(memory_space=pltpu.VMEM)] * 8,
        out_specs=[pl.BlockSpec(memory_space=pl.ANY)] * 5,
        scratch_shapes=[flat, flat, dma((3,)), dma((2, heads))],
        compiler_params=pltpu.CompilerParams(vmem_limit_bytes=8 * 1024 * 1024),
    )(*held)


def solution(mesh):
    tokens = P(("grp", "ctx"), "head")
    states = P(("grp", "head"), None, None)
    return jax.shard_map(
        functools.partial(shards, mesh.shape["ctx"]),
        mesh=mesh,
        in_specs=(tokens, tokens, tokens, states, tokens),
        out_specs=(tokens, tokens, tokens, tokens, states),
        check_vma=False,
    )
```

```python
import functools

import jax
import jax.numpy as jnp
from jax import lax
from jax.experimental import pallas as pl
from jax.experimental.pallas import tpu as pltpu
from jax.sharding import PartitionSpec as P

F32 = jnp.float32
BF16 = jnp.bfloat16
MESH = pl.DeviceIdType.MESH
CHUNK = 256


def nn(a, b):
    return lax.dot_general(a, b, (((1,), (0,)), ((), ())), preferred_element_type=F32)


def nt(a, b):
    return lax.dot_general(a, b, (((1,), (1,)), ((), ())), preferred_element_type=F32)


def tn(a, b):
    return lax.dot_general(a, b, (((0,), (0,)), ((), ())), preferred_element_type=F32)


def kernel(
    n, heads, dim, rows,
    q_hbm, k_hbm, v_hbm, i_hbm, g_hbm,
    out, dq, sg, k, v, acc_a, acc_b, suf,
    q, g, init, score, da, cum, gcum, pre, state, grad,
    p1_in, p2_out, p2_in, p3_out, p3_in,
    b1_in, b2_out, b2_in, b3_out, b3_in, t_out, t_in,
    sem_in, sem_init, one_send, one_recv, two_send, two_recv,
):
    gh = heads // 2
    chips = n // 2
    chunks = rows // CHUNK
    me = lax.axis_index("ctx")
    core = lax.rem(me, 2)
    chip = me // 2
    partner = me + 1 - 2 * core
    peers = [2 * lax.rem(chip + j, chips) + core for j in range(1, chips)]
    mine = core * gh
    other = (1 - core) * gh

    barrier = pltpu.get_barrier_semaphore()
    for device in [partner] + peers:
        pl.semaphore_signal(barrier, inc=1, device_id={"ctx": device}, device_id_type=MESH)

    def strip(h):
        return pl.ds(pl.multiple_of(h * dim, dim), dim)

    def load(which, h):
        src, dst = ((k_hbm, k), (v_hbm, v), (q_hbm, q), (g_hbm, g))[which]
        return pltpu.make_async_copy(
            src.at[:, strip(h)], dst.at[:, strip(h)], sem_in.at[which, h]
        )

    load_init = pltpu.make_async_copy(i_hbm, init, sem_init)

    def issue(first, kinds):
        def step(i, _):
            h = lax.rem(first + i, heads)
            for kind in kinds:
                load(kind, h).start()
            return 0

        lax.fori_loop(0, heads, step, 0)

    issue(other, (0, 1))
    issue(other, (2,))
    load_init.start()
    issue(mine, (3,))
    pl.semaphore_wait(barrier, chips)

    def to_partner(which, src, dst, i):
        return pltpu.make_async_remote_copy(
            src_ref=src, dst_ref=dst,
            send_sem=one_send.at[which, i], recv_sem=one_recv.at[which, i],
            device_id={"ctx": partner}, device_id_type=MESH,
        )

    def to_peer(which, j, src, dst, i):
        return pltpu.make_async_remote_copy(
            src_ref=src, dst_ref=dst,
            send_sem=two_send.at[which, j, i], recv_sem=two_recv.at[which, j, i],
            device_id={"ctx": peers[j]}, device_id_type=MESH,
        )

    def p1(i):
        return to_partner(0, state.at[other + i], p1_in.at[i], i)

    def p2(j, i):
        return to_peer(0, j, p2_out.at[i], p2_in.at[j, i], i)

    def p3(i):
        return to_partner(1, p3_out.at[i], p3_in.at[i], i)

    def b1(i):
        return to_partner(2, grad.at[mine + i], b1_in.at[i], i)

    def b2(j, i):
        return to_peer(1, j, b2_out.at[i], b2_in.at[j, i], i)

    def b3(i):
        return to_partner(3, b3_out.at[i], b3_in.at[i], i)

    def bt(i):
        return to_partner(4, t_out.at[i], t_in.at[i], i)

    def rc(c):
        return pl.ds(c * CHUNK, CHUNK)

    def states(h):
        load(0, h).wait()
        load(1, h).wait()
        parts = [tn(k[rc(c), strip(h)], v[rc(c), strip(h)]) for c in range(chunks)]
        total = jnp.zeros((dim, dim), F32)
        for c in range(chunks):
            cum[h, c] = total
            total = total + parts[c]
        state[h] = total

    def states_other(i, _):
        states(other + i)
        p1(i).start()
        return 0

    lax.fori_loop(0, gh, states_other, 0)

    def states_mine(i, _):
        states(mine + i)
        p1(i).wait_recv()
        p2_out[i] = state[mine + i] + p1_in[i]
        for j in range(chips - 1):
            p2(j, i).start()
        return 0

    lax.fori_loop(0, gh, states_mine, 0)

    causal = lax.broadcasted_iota(jnp.int32, (CHUNK, CHUNK), 0) >= lax.broadcasted_iota(
        jnp.int32, (CHUNK, CHUNK), 1
    )

    def within(i, _):
        h = lax.rem(other + i, heads)
        load(2, h).wait()
        held = []
        for c in range(chunks):
            raw = nt(q[rc(c), strip(h)], k[rc(c), strip(h)])
            held.append(jnp.where(causal, raw, 0.0).astype(BF16))
            score[h, c] = held[c]
        for c in range(chunks):
            acc_a[rc(c), strip(h)] = nn(held[c], v[rc(c), strip(h)])
        return 0

    lax.fori_loop(0, heads, within, 0, unroll=2)
    load_init.wait()

    def forward(h, prefix):
        load(3, h).wait()
        held = []
        for c in range(chunks):
            at = (rc(c), strip(h))
            pre[h, c] = (prefix + cum[h, c]).astype(BF16)
            held.append(acc_a[at] + nn(q[at], pre[h, c]))
        scale = [
            lax.rsqrt(jnp.mean(a * a, axis=-1, keepdims=True) + 1e-06) for a in held
        ]
        held = [a * inv for a, inv in zip(held, scale)]
        rise = []
        for c in range(chunks):
            at = (rc(c), strip(h))
            out[at] = held[c].astype(BF16)
            rise.append(g[at].astype(F32))
        along = [jnp.mean(u * x, axis=-1, keepdims=True) for u, x in zip(rise, held)]
        for c in range(chunks):
            da[rc(c), strip(h)] = (scale[c] * (rise[c] - held[c] * along[c])).astype(BF16)
        parts = [tn(q[rc(c), strip(h)], da[rc(c), strip(h)]) for c in range(chunks)]
        total = parts[0]
        for part in parts[1:]:
            total = total + part
        grad[h] = total
        for c in range(chunks):
            gcum[h, c] = parts[c]

    zero = jnp.zeros((dim, dim), F32)

    def forward_mine(i, _):
        h = mine + i
        before = zero
        for j in range(chips - 1):
            p2(j, i).wait_recv()
            before = before + jnp.where(chip >= j + 1, p2_in[j, i], 0.0)
        p3_out[i] = before + jnp.where(core == 0, state[h], 0.0)
        p3(i).start()
        forward(h, init[h] + before + jnp.where(core == 1, p1_in[i], 0.0))
        b1(i).start()
        return 0

    lax.fori_loop(0, gh, forward_mine, 0)

    def forward_other(i, _):
        h = other + i
        p3(i).wait_recv()
        forward(h, init[h] + p3_in[i])
        b1(i).wait_recv()
        b2_out[i] = grad[h] + b1_in[i]
        for j in range(chips - 1):
            b2(j, i).start()
        return 0

    lax.fori_loop(0, gh, forward_other, 0)

    def backward(i, _):
        h = lax.rem(mine + i, heads)
        held = []
        for c in range(chunks):
            at = (rc(c), strip(h))
            raw = nt(da[at], v[at])
            held.append(jnp.where(causal, raw, 0.0).astype(BF16))
        for c in range(chunks):
            at = (rc(c), strip(h))
            acc_b[at] = tn(score[h, c], da[at])
        for c in range(chunks):
            at = (rc(c), strip(h))
            dq[at] = (nt(da[at], pre[h, c]) + nn(held[c], k[at])).astype(BF16)
        for c in range(chunks):
            at = (rc(c), strip(h))
            acc_a[at] = tn(held[c], q[at])
        return 0

    split = heads - heads // 4
    lax.fori_loop(0, split, backward, 0, unroll=2)

    def relay(i, _):
        h = other + i
        total = b2_out[i]
        after = zero
        for j in range(chips - 1):
            b2(j, i).wait_recv()
            total = total + b2_in[j, i]
            after = after + jnp.where(chip >= j + 1, 0.0, b2_in[j, i])
        b3_out[i] = after + jnp.where(core == 1, grad[h], 0.0)
        b3(i).start()
        t_out[i] = total
        bt(i).start()
        sg[h] = total
        b2_out_later = after + jnp.where(core == 0, b1_in[i], 0.0)
        grad[h] = b2_out_later
        return 0

    lax.fori_loop(0, gh, relay, 0)
    lax.fori_loop(split, heads, backward, 0, unroll=2)

    def finish(h, suffix):
        for c in reversed(range(chunks)):
            suf[h, c] = suffix.astype(BF16)
            if c:
                suffix = suffix + gcum[h, c]

    def finish_other(i, _):
        finish(other + i, grad[other + i])
        return 0

    lax.fori_loop(0, gh, finish_other, 0)

    def finish_mine(i, _):
        b3(i).wait_recv()
        finish(mine + i, b3_in[i])
        bt(i).wait_recv()
        sg[mine + i] = t_in[i]
        return 0

    lax.fori_loop(0, gh, finish_mine, 0)

    def drain(i, _):
        p1(i).wait_send()
        p3(i).wait_send()
        b1(i).wait_send()
        b3(i).wait_send()
        bt(i).wait_send()
        for j in range(chips - 1):
            p2(j, i).wait_send()
            b2(j, i).wait_send()
        return 0

    lax.fori_loop(0, gh, drain, 0)


def tail(
    heads, dim, rows,
    out, dq, sg, k, v, acc_a, acc_b, suf,
    out_hbm, dq_hbm, dk_hbm, dv_hbm, sg_hbm,
    dk, dv, sem_whole, sem_head,
):
    chunks = rows // CHUNK
    whole = [
        pltpu.make_async_copy(src, dst, sem_whole.at[i])
        for i, (src, dst) in enumerate(((out, out_hbm), (dq, dq_hbm), (sg, sg_hbm)))
    ]
    for copy in whole:
        copy.start()

    def strip(h):
        return pl.ds(pl.multiple_of(h * dim, dim), dim)

    def store(which, h):
        src, dst = ((dk, dk_hbm), (dv, dv_hbm))[which]
        return pltpu.make_async_copy(
            src.at[:, strip(h)], dst.at[:, strip(h)], sem_head.at[which, h]
        )

    def finish(h, _):
        for c in range(chunks):
            at = (pl.ds(c * CHUNK, CHUNK), strip(h))
            s_b = suf[h, c]
            dk[at] = (acc_a[at] + nt(v[at], s_b)).astype(BF16)
            dv[at] = (acc_b[at] + nn(k[at], s_b)).astype(BF16)
        store(0, h).start()
        store(1, h).start()
        return 0

    lax.fori_loop(0, heads, finish, 0, unroll=2)

    def drain(h, _):
        store(0, h).wait()
        store(1, h).wait()
        return 0

    lax.fori_loop(0, heads, drain, 0)
    for copy in whole:
        copy.wait()


def shards(n, queries, keys, values, init_state, out_grad):
    rows, width = queries.shape
    heads, dim, _ = init_state.shape
    gh = heads // 2
    chips = n // 2
    chunks = rows // CHUNK
    far = max(chips - 1, 1)
    flat = pltpu.VMEM((rows, width), BF16)
    wide = pltpu.VMEM((rows, width), F32)
    group = pltpu.VMEM((gh, dim, dim), F32)
    every = pltpu.VMEM((heads, dim, dim), F32)
    peers = pltpu.VMEM((far, gh, dim, dim), F32)
    dma = pltpu.SemaphoreType.DMA
    held = pl.pallas_call(
        functools.partial(kernel, n, heads, dim, rows),
        out_shape=[
            flat, flat, every, flat, flat, wide, wide,
            pltpu.VMEM((heads, chunks, dim, dim), BF16),
        ],
        in_specs=[pl.BlockSpec(memory_space=pltpu.HBM)] * 5,
        out_specs=[pl.BlockSpec(memory_space=pltpu.VMEM)] * 8,
        scratch_shapes=[
            flat, flat, every,
            pltpu.VMEM((heads, chunks, CHUNK, CHUNK), BF16),
            flat,
            pltpu.VMEM((heads, chunks, dim, dim), F32),
            pltpu.VMEM((heads, chunks, dim, dim), F32),
            pltpu.VMEM((heads, chunks, dim, dim), BF16),
            every, every,
            group, group, peers, group, group,
            group, group, peers, group, group, group, group,
            dma((4, heads)), dma,
            dma((5, gh)), dma((5, gh)),
            dma((2, far, gh)), dma((2, far, gh)),
        ],
        compiler_params=pltpu.CompilerParams(
            collective_id=0, has_side_effects=True, vmem_limit_bytes=46 * 1024 * 1024
        ),
    )(queries, keys, values, init_state, out_grad)
    flat_out = jax.ShapeDtypeStruct((rows, width), BF16)
    return pl.pallas_call(
        functools.partial(tail, heads, dim, rows),
        out_shape=[flat_out] * 4 + [jax.ShapeDtypeStruct((heads, dim, dim), F32)],
        in_specs=[pl.BlockSpec(memory_space=pltpu.VMEM)] * 8,
        out_specs=[pl.BlockSpec(memory_space=pl.ANY)] * 5,
        scratch_shapes=[flat, flat, dma((3,)), dma((2, heads))],
        compiler_params=pltpu.CompilerParams(vmem_limit_bytes=8 * 1024 * 1024),
    )(*held)


def solution(mesh):
    tokens = P(("grp", "ctx"), "head")
    states = P(("grp", "head"), None, None)
    return jax.shard_map(
        functools.partial(shards, mesh.shape["ctx"]),
        mesh=mesh,
        in_specs=(tokens, tokens, tokens, states, tokens),
        out_specs=(tokens, tokens, tokens, tokens, states),
        check_vma=False,
    )
```
